32 devices in a mesh: seq: 8 (over z, y), band: 4 (over x, core).
Axes of the slice: x: 2, y: 2, z: 4, core: 2. Of those that a mesh axis runs over, the one named last changes fastest.
Arguments:
- tokens: bfloat16 [16, 4, 16, 16, 768], P('seq', None, 'band'), may hold values from -6 to 6
- slot_ids: int32 [16, 4], P('seq'), may hold values from 0 to 3, as said below
- cotangent: bfloat16 [16, 4, 16, 16, 768], P('seq', None, 'band'), may hold values from -6 to 6
- ln1_gain: bfloat16 [768], replicated, may hold values from 0.5 to 1.5
- ln1_bias: bfloat16 [768], replicated, may hold values from -1.5 to 1.5
- w_query: bfloat16 [768, 768], replicated, may hold values from -0.21875 to 0.21875
- b_query: bfloat16 [768], replicated, may hold values from -2.5 to 2.5
- w_key: bfloat16 [768, 768], replicated, may hold values from -0.21875 to 0.21875
- w_value: bfloat16 [768, 768], replicated, may hold values from -0.21875 to 0.21875
- b_value: bfloat16 [768], replicated, may hold values from -2.5 to 2.5
- w_out: bfloat16 [768, 768], replicated, may hold values from -2 to 2
- b_out: bfloat16 [768], replicated, may hold values from -1.5 to 1.5
- ln2_gain: bfloat16 [768], replicated, may hold values from 0.5 to 1.5
- ln2_bias: bfloat16 [768], replicated, may hold values from -1.5 to 1.5
- w_up: bfloat16 [768, 3072], replicated, may hold values from -0.21875 to 0.21875
- b_up: bfloat16 [3072], replicated, may hold values from -2.5 to 2.5
- w_down: bfloat16 [3072, 768], replicated, may hold values from -0.109375 to 0.109375
- b_down: bfloat16 [768], replicated, may hold values from -1.5 to 1.5
Outputs:
- output: bfloat16 [16, 4, 16, 16, 768], P('seq', None, 'band')
- input_grad: bfloat16 [16, 4, 16, 16, 768], P('seq', None, 'band')
- grad_ln1_gain: float32 [768], P('seq')
- grad_ln1_bias: float32 [768], P('seq')
- grad_w_query: float32 [768, 768], P('seq')
- grad_b_query: float32 [768], P('seq')
- grad_w_key: float32 [768, 768], P('seq')
- grad_w_value: float32 [768, 768], P('seq')
- grad_b_value: float32 [768], P('seq')
- grad_w_out: float32 [768, 768], P('seq')
- grad_b_out: float32 [768], P('seq')
- grad_ln2_gain: float32 [768], P('seq')
- grad_ln2_bias: float32 [768], P('seq')
- grad_w_up: float32 [768, 3072], P('seq')
- grad_b_up: float32 [3072], P('seq')
- grad_w_down: float32 [3072, 768], P('seq')
- grad_b_down: float32 [768], P('seq')
The draws below stay inside these ranges and needn't reach their ends.
Inputs may be any that keep to these rules, and one draw needn't show every extreme that they name: `slot_ids`: A token attends to all tokens of its sequence whose image slot carries the same id; several slots of one sequence may share an id.
All inputs are finite; a program needn't handle non-finite values.
Results may differ from the reference program's by a relative error of at most 0.017.
Values may be sent and summed in bfloat16 or wider, within the bound.
A program may use at most 256 MiB of HBM per device.

```python
import math
import jax
import jax.numpy as jnp
from jax import lax

D = 768
HEADS = 16
HEAD_DIM = 48
FF = 3072
IMAGES = 4
GRID_ROWS = 16
GRID_COLS = 16
SEQS = 16


def draw_slot_ids(key, part):
    labels = jax.random.randint(key, (SEQS, IMAGES), 0, IMAGES)
    labels = labels.at[0, 0].set(0).at[0, IMAGES - 1].set(IMAGES - 1)
    return labels.astype(jnp.int32)


def levels(stream_key, dims, shards, smallest, largest):
    loudness = 1.0
    for position, parts in shards:
        draws = jax.random.uniform(jax.random.fold_in(jax.random.fold_in(stream_key, 6), position), (parts,), jnp.float32, smallest / len(shards), largest / len(shards))
        loudness = loudness * jnp.repeat(jnp.exp(draws), dims[position] // parts).reshape((-1,) + (1,) * (len(dims) - 1 - position))
    return loudness


def normal_values(own_key, extent, width, reach, shards=(), held_as=jnp.bfloat16):
    entries = jax.random.normal(own_key, extent, jnp.float32) * width
    if len(shards) > 0:
        entries = levels(own_key, extent, shards, -0.22, 0.18) * entries
    return jnp.clip(entries, min=-reach, max=reach).astype(held_as)


def setup_inputs(seed: int = 0) -> dict:
    key_list = jax.random.split(jax.random.key(seed), 19)
    tokens = normal_values(key_list[0], (SEQS, IMAGES, GRID_ROWS, GRID_COLS, D), 1.0, 6.0, ((0, 8), (2, 4)))
    slot_ids = draw_slot_ids(jax.random.fold_in(key_list[18], 71), 0)
    cotangent = normal_values(key_list[2], (SEQS, IMAGES, GRID_ROWS, GRID_COLS, D), 1.0, 6.0, ((0, 8), (2, 4)))
    ln1_gain = jnp.clip(1.0 + 0.1 * jax.random.normal(key_list[3], (D,), jnp.float32), 0.5, 1.5).astype(jnp.bfloat16)
    ln1_bias = normal_values(key_list[4], (D,), 0.3, 1.5)
    w_query = normal_values(key_list[5], (D, D), D ** -0.5, 0.21875)
    b_query = normal_values(key_list[6], (D,), 0.5, 2.5)
    w_key = normal_values(key_list[7], (D, D), D ** -0.5, 0.21875)
    w_value = normal_values(key_list[8], (D, D), D ** -0.5, 0.21875)
    b_value = normal_values(key_list[9], (D,), 0.5, 2.5)
    w_out = normal_values(key_list[10], (D, D), 8 ** -0.5, 2.0)
    b_out = normal_values(key_list[11], (D,), 0.3, 1.5)
    ln2_gain = jnp.clip(1.0 + 0.1 * jax.random.normal(key_list[12], (D,), jnp.float32), 0.5, 1.5).astype(jnp.bfloat16)
    ln2_bias = normal_values(key_list[13], (D,), 0.3, 1.5)
    w_up = normal_values(key_list[14], (D, FF), D ** -0.5, 0.21875)
    b_up = normal_values(key_list[15], (FF,), 0.5, 2.5)
    w_down = normal_values(key_list[16], (FF, D), FF ** -0.5, 0.109375)
    b_down = normal_values(key_list[17], (D,), 0.3, 1.5)
    return dict(tokens=tokens, slot_ids=slot_ids, cotangent=cotangent, ln1_gain=ln1_gain, ln1_bias=ln1_bias, w_query=w_query, b_query=b_query, w_key=w_key, w_value=w_value, b_value=b_value, w_out=w_out, b_out=b_out, ln2_gain=ln2_gain, ln2_bias=ln2_bias, w_up=w_up, b_up=b_up, w_down=w_down, b_down=b_down)


EPSILON = 1e-05
HIGHEST = lax.Precision.HIGHEST

@jax.custom_vjp
def low(v):
    return lax.optimization_barrier(v.astype(jnp.bfloat16)).astype(jnp.float32)

@jax.custom_vjp
def low_back(v):
    return v

def low_keep(v):
    return (low(v), None)

def low_pass(kept, grad):
    return (grad,)

def back_keep(v):
    return (v, None)

def back_low(kept, grad):
    return (low(grad),)
low.defvjp(low_keep, low_pass)
low_back.defvjp(back_keep, back_low)

def layer_norm(inputs, gain_vec, bias_vec):
    centre = lax.optimization_barrier(jnp.mean(inputs, axis=-1, keepdims=True))
    centred = inputs - centre
    spread = lax.optimization_barrier(jnp.mean(centred * centred, axis=-1, keepdims=True))
    return centred * lax.rsqrt(spread + EPSILON) * gain_vec + bias_vec

def product(left, right):
    return jnp.dot(left, right, precision=HIGHEST)

def forward(inputs, token_slots, ln1_gain, ln1_bias, w_query, b_query, w_key, w_value, b_value, w_out, b_out, ln2_gain, ln2_bias, w_up, b_up, w_down, b_down):
    length = inputs.shape[0]
    score_scale = 1.0 / math.sqrt(HEAD_DIM)
    normed = low(layer_norm(inputs, ln1_gain, ln1_bias))
    queries = low(low_back(product(normed, w_query) + b_query)).reshape(length, HEADS, HEAD_DIM)
    key_rows = low(low_back(product(normed, w_key))).reshape(length, HEADS, HEAD_DIM)
    value_rows = low(low_back(product(normed, w_value) + b_value)).reshape(length, HEADS, HEAD_DIM)
    scores = jnp.einsum('qhd,khd->hqk', queries, key_rows, precision=HIGHEST) * score_scale
    scores = low_back(scores)
    same_image = token_slots[:, None] == token_slots[None, :]
    scores = jnp.where(same_image[None], scores, -jnp.inf)
    row_max = lax.optimization_barrier(jnp.max(scores, axis=-1, keepdims=True))
    exp_scores = jnp.exp(scores - row_max)
    weights = low(exp_scores / lax.optimization_barrier(jnp.sum(exp_scores, axis=-1, keepdims=True)))
    attended = jnp.einsum('hqk,khd->qhd', weights, value_rows, precision=HIGHEST).reshape(length, D)
    attended = low(low_back(attended))
    middle = inputs + low_back(product(attended, w_out) + b_out)
    normed_two = low(layer_norm(middle, ln2_gain, ln2_bias))
    hidden_pre = low_back(product(normed_two, w_up) + b_up)
    hidden = low(jax.nn.gelu(hidden_pre, approximate=False))
    return middle + low_back(product(hidden, w_down) + b_down)

def reference(tokens, slot_ids, cotangent, ln1_gain, ln1_bias, w_query, b_query, w_key, w_value, b_value, w_out, b_out, ln2_gain, ln2_bias, w_up, b_up, w_down, b_down):
    params = tuple((member.astype(jnp.float32) for member in (ln1_gain, ln1_bias, w_query, b_query, w_key, w_value, b_value, w_out, b_out, ln2_gain, ln2_bias, w_up, b_up, w_down, b_down)))
    seq_total = tokens.shape[0]
    length = IMAGES * GRID_ROWS * GRID_COLS
    flat_tokens = tokens.reshape(seq_total, length, D)
    flat_cot = cotangent.reshape(seq_total, length, D)
    token_slots = jnp.repeat(slot_ids.astype(jnp.int32), GRID_ROWS * GRID_COLS, axis=1)
    zeros = tuple((jnp.zeros(member.shape, jnp.float32) for member in params))

    def step(totals, entry):
        seq_tokens, seq_slots, seq_cot = entry

        def run(inputs, *weights_all):
            return forward(inputs, seq_slots, *weights_all)
        result, pull = jax.vjp(run, seq_tokens.astype(jnp.float32), *params)
        grads = pull(seq_cot.astype(jnp.float32))
        updated = tuple((first + second for first, second in zip(totals, grads[1:])))
        return (updated, (result.astype(jnp.bfloat16), grads[0].astype(jnp.bfloat16)))
    totals, (results, input_grads) = lax.scan(step, zeros, (flat_tokens, token_slots, flat_cot))
    return (results.reshape(tokens.shape), input_grads.reshape(tokens.shape), totals[0], totals[1], totals[2], totals[3], totals[4], totals[5], totals[6], totals[7], totals[8], totals[9], totals[10], totals[11], totals[12], totals[13], totals[14])
```

```python
import functools
import math

import jax
import jax.numpy as jnp
from jax import lax
from jax.experimental import pallas as pl
from jax.experimental.pallas import tpu as pltpu
from jax.sharding import PartitionSpec as P

HEADS = 16
HEAD_DIM = 48
IMAGES = 4
EPSILON = 1e-05
F32 = jnp.float32
BF16 = jnp.bfloat16
MESH = pl.DeviceIdType.MESH
LN2 = math.log(2.0)
QUERY_SCALE = 1.0 / (math.sqrt(HEAD_DIM) * LN2)
GROUPS = 8


def dot_nn(a, b):
    return lax.dot_general(a, b, (((1,), (0,)), ((), ())), preferred_element_type=F32)


def dot_nt(a, b):
    return lax.dot_general(a, b, (((1,), (1,)), ((), ())), preferred_element_type=F32)


def dot_tn(a, b):
    return lax.dot_general(a, b, (((0,), (0,)), ((), ())), preferred_element_type=F32)


def dot_tt(a, b):
    return lax.dot_general(a, b, (((0,), (1,)), ((), ())), preferred_element_type=F32)


class Place:
    def __init__(self, seq_size):
        self.stride = seq_size // GROUPS
        band = lax.axis_index("band")
        self.band = band
        self.core = band % 2
        self.chip = band // 2
        self.seq = lax.axis_index("seq")
        group = self.seq // self.stride
        self.bits = (group % 2, (group // 2) % 2, group // 4)

    def partner(self, way):
        if way == "core":
            return {"band": self.band + 1 - 2 * self.core}
        if way == "x":
            return {"band": self.band + 2 - 4 * self.chip}
        bit = self.bits[way]
        return {"seq": self.seq + (1 - 2 * bit) * (self.stride << way)}


def greet(place, ways):
    barrier = pltpu.get_barrier_semaphore()
    for way in ways:
        pl.semaphore_signal(barrier, inc=1, device_id=place.partner(way), device_id_type=MESH)
    pl.semaphore_wait(barrier, len(ways))


class Links:
    def __init__(self, place, send, recv):
        self.place, self.send, self.recv, self.next = place, send, recv, 0

    def copy(self, src, dst, way):
        slot = self.next
        self.next += 1
        return pltpu.make_async_remote_copy(
            src_ref=src,
            dst_ref=dst,
            send_sem=self.send.at[slot],
            recv_sem=self.recv.at[slot],
            device_id=self.place.partner(way),
            device_id_type=MESH,
        )


def norm_parts(rows):
    centred = rows - jnp.mean(rows, axis=-1, keepdims=True)
    scale = lax.rsqrt(jnp.mean(centred * centred, axis=-1, keepdims=True) + EPSILON)
    return centred * scale, scale


def norm_back(hat, scale, gain, grad):
    inner = grad * gain
    return scale * (
        inner
        - jnp.mean(inner, axis=-1, keepdims=True)
        - hat * jnp.mean(inner * hat, axis=-1, keepdims=True)
    )


GAIN_1, BIAS_1, B_QUERY, B_VALUE, B_OUT, GAIN_2, BIAS_2, B_DOWN, B_UP = range(9)
VECTORS = 16


def vector(ref, row):
    return ref[row : row + 1, :].astype(F32)


def vector_columns(ref):
    rows = lax.broadcasted_iota(jnp.int32, (VECTORS, 128), 0)
    lanes = lax.broadcasted_iota(jnp.int32, (VECTORS, 128), 1)
    return dot_tn(ref[...], jnp.where(rows == lanes, 1.0, 0.0).astype(BF16))


def set_mask(mask_ref, slot_ref, place):
    queries = mask_ref.shape[1]
    image = lax.broadcasted_iota(jnp.int32, (1, queries), 1) // (queries // 2 // IMAGES) % IMAGES
    ids = [slot_ref[place.chip, j] for j in range(IMAGES)]
    own = jnp.full((1, queries), 0, jnp.int32) + ids[0]
    for j in range(1, IMAGES):
        own = jnp.where(image == j, ids[j], own)
    for j in range(IMAGES):
        mask_ref[j : j + 1, :] = jnp.where(own == ids[j], 0.0, jnp.inf)


def front_kernel(
    seq_size,
    tok_ref,
    cot_ref,
    wq_hbm,
    wk_hbm,
    wv_hbm,
    vec_ref,
    slot_ref,
    x_ref,
    g_ref,
    a_ref,
    q_ref,
    k_ref,
    v_ref,
    o_ref,
    lse_ref,
    wq_ref,
    wk_ref,
    wv_ref,
    p_ref,
    mask_ref,
    load_sem,
    send_sem,
    recv_sem,
):
    place = Place(seq_size)
    links = Links(place, send_sem, recv_sem)
    half = x_ref.shape[0] // 2
    gain, bias = vector(vec_ref, GAIN_1), vector(vec_ref, BIAS_1)
    rows = 2 * half
    loads = [
        pltpu.make_async_copy(tok_ref.at[place.chip], x_ref.at[pl.ds(0, half)], load_sem.at[0]),
        pltpu.make_async_copy(wq_hbm, wq_ref, load_sem.at[1]),
        pltpu.make_async_copy(wk_hbm, wk_ref, load_sem.at[2]),
        pltpu.make_async_copy(wv_hbm, wv_ref, load_sem.at[3]),
        pltpu.make_async_copy(cot_ref.at[place.chip], g_ref.at[pl.ds(0, half)], load_sem.at[4]),
    ]
    for load in loads:
        load.start()
    greet(place, ("x", "core"))
    token_swap = links.copy(tok_ref.at[1 - place.chip], x_ref.at[pl.ds(half, half)], "x")
    cot_swap = links.copy(cot_ref.at[1 - place.chip], g_ref.at[pl.ds(half, half)], "x")
    token_swap.start()
    cot_swap.start()
    set_mask(mask_ref, slot_ref, place)
    columns = vector_columns(vec_ref)
    bq, bv = columns[:, B_QUERY : B_QUERY + 1], columns[:, B_VALUE : B_VALUE + 1]
    shares = []
    for part in range(2):
        span = pl.ds(part * half, half)
        if part == 0:
            for load in loads[:4]:
                load.wait()
        else:
            token_swap.wait_recv()
        hat, _ = norm_parts(x_ref[span, :].astype(F32))
        normed = (hat * gain + bias).astype(BF16)
        a_ref[span, :] = normed
        k_ref[:, span] = dot_tt(wk_ref[...], normed).astype(BF16)
        v_ref[:, span] = (dot_tt(wv_ref[...], normed) + bv).astype(BF16)
        far = pl.ds(rows + part * half, half)
        for ref in (k_ref, v_ref):
            share = links.copy(ref.at[:, span], ref.at[:, far], "core")
            share.start()
            shares.append(share)
        q_ref[:, span] = ((dot_tt(wq_ref[...], normed) + bq) * QUERY_SCALE).astype(BF16)
    for share in shares:
        share.wait_recv()
    block = half // IMAGES
    keys = k_ref.shape[1]

    def head(h, _):
        feats = pl.ds(pl.multiple_of(h * HEAD_DIM, 16), HEAD_DIM)
        scores = dot_tn(k_ref[feats, :], q_ref[feats, :])
        top = None
        for image in range(IMAGES):
            best = None
            for b in range(image, keys // block, IMAGES):
                one = jnp.max(scores[b * block : (b + 1) * block], axis=0, keepdims=True)
                best = one if best is None else jnp.maximum(best, one)
            best = best - mask_ref[image : image + 1, :]
            top = best if top is None else jnp.maximum(top, best)
        total = None
        for b in range(keys // block):
            image = b % IMAGES
            weight = jnp.exp2(
                scores[b * block : (b + 1) * block] - (top + mask_ref[image : image + 1, :])
            )
            one = jnp.sum(weight, axis=0, keepdims=True)
            total = one if total is None else total + one
            p_ref[pl.ds(b * block, block), :] = weight.astype(BF16)
        out = dot_nn(v_ref[feats, :], p_ref[...])
        o_ref[feats, :] = (out / total).astype(BF16)
        lse_ref[h] = top + jnp.log2(total)
        return 0

    lax.fori_loop(0, HEADS, head, 0)
    token_swap.wait_send()
    cot_swap.wait()
    loads[4].wait()
    for share in shares:
        share.wait_send()


def any_spec():
    return pl.BlockSpec(memory_space=pl.ANY)


def vmem_spec():
    return pl.BlockSpec(memory_space=pltpu.VMEM)


def smem_spec():
    return pl.BlockSpec(memory_space=pltpu.SMEM)


def front(seq_size, tokens, cotangent, wq, wk, wv, vectors, slot_ids):
    rows, width = 2 * tokens.shape[1], tokens.shape[2]
    shape = jax.ShapeDtypeStruct
    return pl.pallas_call(
        functools.partial(front_kernel, seq_size),
        out_shape=(
            shape((rows, width), BF16),
            shape((rows, width), BF16),
            shape((rows, width), BF16),
            shape((width, rows), BF16),
            shape((width, 2 * rows), BF16),
            shape((width, 2 * rows), BF16),
            shape((width, rows), BF16),
            shape((HEADS, 1, rows), F32),
        ),
        in_specs=[any_spec()] * 5 + [vmem_spec(), smem_spec()],
        out_specs=[vmem_spec()] * 8,
        scratch_shapes=[
            pltpu.VMEM((width, width), BF16),
            pltpu.VMEM((width, width), BF16),
            pltpu.VMEM((width, width), BF16),
            pltpu.VMEM((2 * rows, rows), BF16),
            pltpu.VMEM((8, rows), F32),
            pltpu.SemaphoreType.DMA((5,)),
            pltpu.SemaphoreType.DMA((6,)),
            pltpu.SemaphoreType.DMA((6,)),
        ],
        compiler_params=pltpu.CompilerParams(collective_id=1, has_side_effects=True),
        name="front",
    )(tokens, cotangent, wq, wk, wv, vectors, slot_ids)


class Item:
    def __init__(self, links, src, bufs, x_first, write):
        place = links.place
        b0, b1, b2 = place.bits
        self.src, self.bufs, self.x_first, self.write = src, bufs, x_first, write
        if x_first:
            r0, r1, r2, r3, fin, other = bufs
            half = src.shape[-2] // 2
            self.mine = pl.ds(pl.multiple_of(place.chip * half, 16), half)
            away = pl.ds(pl.multiple_of((1 - place.chip) * half, 16), half)
            self.keep = [
                src.at[:, :, :, self.mine],
                r0.at[:, :, b0],
                r1.at[:, b1],
                r2.at[b2],
            ]
            self.sends = [
                links.copy(src.at[:, :, :, away], r0, "x"),
                links.copy(r0.at[:, :, 1 - b0], r1, 0),
                links.copy(r1.at[:, 1 - b1], r2, 1),
                links.copy(r2.at[1 - b2], r3, 2),
                links.copy(r3, fin.at[self.mine], "x"),
                links.copy(fin, other, "core"),
            ]
        else:
            r0, r1, r2, r3, fin, other = bufs
            self.keep = [src.at[:, :, b0], r0.at[:, b1], r1.at[b2]]
            self.sends = [
                links.copy(src.at[:, :, 1 - b0], r0, 0),
                links.copy(r0.at[:, 1 - b1], r1, 1),
                links.copy(r1.at[1 - b2], r2, 2),
                links.copy(r2, r3, "x"),
                links.copy(fin, other, "core"),
            ]
        self.last = len(self.sends)

    def step(self, index):
        if index > 0:
            self.sends[index - 1].wait_recv()
        if 0 < index <= len(self.keep):
            add_to(self.bufs[index - 1], self.keep[index - 1])
        fin, other = self.bufs[4:]
        if self.x_first and index == 4:
            fin[self.mine] = self.bufs[3][...]
        if not self.x_first and index == 4:
            fin[...] = (self.bufs[2][...].astype(F32) + self.bufs[3][...].astype(F32)).astype(BF16)
        if index == self.last:
            self.write(fin, other)
        else:
            self.sends[index].start()

    def finish(self):
        for send in self.sends:
            send.wait_send()


def add_to(ref, more):
    ref[...] = (ref[...].astype(F32) + more[...].astype(F32)).astype(BF16)


def item_buffers(rows, columns, x_first):
    part = rows // 2 if x_first else rows
    if x_first:
        dims = [(2, 2, 2, part), (2, 2, part), (2, part), (part,), (rows,), (rows,)]
    else:
        dims = [(2, 2, part), (2, part), (part,), (part,), (rows,), (rows,)]
    return [pltpu.VMEM(d + (columns,), BF16) for d in dims]


def item_copies(x_first):
    return 6 if x_first else 5


def column_writer(out_ref, place, start, columns, half):
    def write(fin, other):
        mine = pl.multiple_of(place.core * half + start, 128)
        away = pl.multiple_of((1 - place.core) * half + start, 128)
        out_ref[:, pl.ds(mine, columns)] = fin[...].astype(F32)
        out_ref[:, pl.ds(away, columns)] = other[...].astype(F32)

    return write


DOWN_PIECES = 3
UP_PIECES = 4
BACK_ITEMS = ("D0", "D1", "D2", "U0", "U1", "U2", "U3", "O")
BACK_PLAN = (
    (("D0", 0), ("U0", 0),),
    (),
    (("U1", 0),),
    (("D1", 0),),
    (("U0", 1),),
    (("D0", 1), ("share", 0),),
    (),
    (("U0", 2), ("U1", 1), ("O", 0), ("D2", 0), ("sum", 0),),
    (),
    (("D0", 2), ("D1", 1), ("share", 1),),
    (("U0", 3), ("U1", 2),),
    (("D0", 3), ("O", 1), ("U2", 0), ("out", 0), ("sum", 1),),
    (("D2", 1),),
    (("D0", 4), ("U0", 4), ("U1", 3), ("D1", 2), ("share", 2),),
    (("U0", 5), ("O", 2),),
    (("D1", 3), ("sum", 2),),
    (("share", 3), ("U2", 1), ("U3", 0), ("O", 3), ("out", 1), ("sum", 3), ("D0", 5), ("D1", 4), ("U1", 4), ("D2", 2), ("D0", 6), ("U1", 5), ("O", 4), ("U2", 2), ("D1", 5), ("O", 5), ("D2", 3), ("D1", 6), ("U2", 3), ("U3", 1), ("D2", 4), ("U2", 4), ("D2", 5), ("U3", 2), ("U2", 5), ("D2", 6), ("U3", 3), ("U3", 4), ("U3", 5),),
)
KEY_BLOCKS = 4


def back_kernel(seq_size, *refs):
    refs = list(refs)
    take = lambda count: [refs.pop(0) for _ in range(count)]
    slot_ref, q_ref, k_ref, v_ref, do_ref, lse_ref, delta_ref, fwd_ref = take(8)
    down_ref, up_ref, wout_ref = take(3)
    dq_ref, dk_ref, dv_ref, out_ref, gd_ref, gu_ref, go_ref = take(7)
    mask_ref, far_dk, far_dv, got_dk, got_dv, send_sem, recv_sem = take(7)
    place = Place(seq_size)
    links = Links(place, send_sem, recv_sem)
    width, rows = q_ref.shape
    half = rows // 2
    items = {}
    for piece in range(DOWN_PIECES):
        columns = down_ref.shape[-1]
        items["D%d" % piece] = Item(
            links,
            down_ref.at[piece],
            take(6),
            True,
            column_writer(gd_ref, place, piece * columns, columns, DOWN_PIECES * columns),
        )
    for piece in range(UP_PIECES):
        columns = up_ref.shape[-1]
        items["U%d" % piece] = Item(
            links,
            up_ref.at[piece],
            take(6),
            False,
            column_writer(gu_ref, place, piece * columns, columns, UP_PIECES * columns),
        )
    columns = wout_ref.shape[-1]
    items["O"] = Item(
        links, wout_ref, take(6), False, column_writer(go_ref, place, 0, columns, columns)
    )
    greet(place, ("core", "x", 0, 1, 2))
    back_swap = links.copy(fwd_ref.at[pl.ds(half, half)], out_ref.at[place.chip], "x")
    group_rows = width // 4
    shares = []
    for group in range(4):
        span = pl.ds(group * group_rows, group_rows)
        shares.append(
            [
                links.copy(far_dk.at[span], got_dk.at[span], "core"),
                links.copy(far_dv.at[span], got_dv.at[span], "core"),
            ]
        )
    out_ref[place.chip] = fwd_ref[0:half, :]
    set_mask(mask_ref, slot_ref, place)

    def run(name, step):
        if name == "out":
            if step == 0:
                back_swap.start()
            else:
                back_swap.wait_recv()
        elif name == "share":
            for share in shares[step]:
                share.start()
        elif name == "sum":
            span = pl.ds(step * group_rows, group_rows)
            for share in shares[step]:
                share.wait_recv()
            add_to(dk_ref.at[span], got_dk.at[span])
            add_to(dv_ref.at[span], got_dv.at[span])
        else:
            items[name].step(step)

    keys = 2 * rows
    block = keys // KEY_BLOCKS
    small = half // IMAGES

    def head(h, _):
        for turn, acts in enumerate(BACK_PLAN[:HEADS]):
            if acts:

                @pl.when(h == turn)
                def _(acts=acts):
                    for act in acts:
                        run(*act)

        feats = pl.ds(pl.multiple_of(h * HEAD_DIM, 16), HEAD_DIM)
        query, dout = q_ref[feats, :], do_ref[feats, :]
        lse, delta = lse_ref[h], delta_ref[h]
        tops = [lse + mask_ref[j : j + 1, :] for j in range(IMAGES)]
        dquery = None
        for b in range(KEY_BLOCKS):
            span = slice(b * block, (b + 1) * block)
            key, value = k_ref[feats, span], v_ref[feats, span]
            scores = dot_tn(key, query)
            parts = []
            for i in range(block // small):
                image = (b * (block // small) + i) % IMAGES
                parts.append(jnp.exp2(scores[i * small : (i + 1) * small] - tops[image]))
            weights = jnp.concatenate(parts, axis=0)
            dscores = (weights * (dot_tn(value, dout) - delta)).astype(BF16)
            weights = weights.astype(BF16)
            dvalue = dot_nt(dout, weights).astype(BF16)
            dkey = (dot_nt(query, dscores) * LN2).astype(BF16)
            one = dot_nn(key, dscores)
            dquery = one if dquery is None else dquery + one
            if b < KEY_BLOCKS // 2:
                dk_ref[feats, span] = dkey
                dv_ref[feats, span] = dvalue
            else:
                there = slice(b * block - rows, (b + 1) * block - rows)
                far_dk[feats, there] = dkey
                far_dv[feats, there] = dvalue
        dq_ref[feats, :] = (dquery * (1.0 / math.sqrt(HEAD_DIM))).astype(BF16)
        return 0

    lax.fori_loop(0, HEADS, head, 0)
    for acts in BACK_PLAN[HEADS:]:
        for act in acts:
            run(*act)
    back_swap.wait_send()
    for group in shares:
        for share in group:
            share.wait_send()
    for name in BACK_ITEMS:
        items[name].finish()


def back(seq_size, slot_ids, q, k, v, do, lse, delta, fwd, down, up, wout):
    width, rows = q.shape
    shape = jax.ShapeDtypeStruct
    pieces = [(down.shape[-2:], True)] * DOWN_PIECES + [(up.shape[-2:], False)] * UP_PIECES
    pieces.append((wout.shape[-2:], False))
    copies = sum(item_copies(first) for _, first in pieces) + 1 + 8
    buffers = []
    for (r, c), first in pieces:
        buffers += item_buffers(r, c, first)
    return pl.pallas_call(
        functools.partial(back_kernel, seq_size),
        out_shape=(
            shape((width, rows), BF16),
            shape((width, rows), BF16),
            shape((width, rows), BF16),
            shape((2, rows // 2, width), BF16),
            shape((down.shape[-2], 2 * DOWN_PIECES * down.shape[-1]), F32),
            shape((up.shape[-2], 2 * UP_PIECES * up.shape[-1]), F32),
            shape((wout.shape[-2], 2 * wout.shape[-1]), F32),
        ),
        in_specs=[smem_spec()] + [vmem_spec()] * 10,
        out_specs=[vmem_spec()] * 7,
        scratch_shapes=[
            pltpu.VMEM((8, rows), F32),
            pltpu.VMEM((width, rows), BF16),
            pltpu.VMEM((width, rows), BF16),
            pltpu.VMEM((width, rows), BF16),
            pltpu.VMEM((width, rows), BF16),
            pltpu.SemaphoreType.DMA((copies,)),
            pltpu.SemaphoreType.DMA((copies,)),
        ]
        + buffers,
        compiler_params=pltpu.CompilerParams(collective_id=2, has_side_effects=True),
        name="back",
    )(slot_ids, q, k, v, do, lse, delta, fwd, down, up, wout)


LATE_PLAN = (
    ("sum", 0),
    ("V", 1),
    ("sum", 1),
    ("K", 1),
    ("V", 2),
    ("sum", 2),
    ("Q", 1),
    ("V", 3),
    ("K", 2),
    ("sum", 3),
    ("Q", 2),
    ("V", 4),
    ("K", 3),
    ("sum", 4),
    ("Q", 3),
    ("K", 4),
    ("V", 5),
    ("sum", 5),
    ("Q", 4),
    ("K", 5),
    ("Q", 5),
    ("K", 6),
)


def late_kernel(seq_size, *refs):
    refs = list(refs)
    take = lambda count: [refs.pop(0) for _ in range(count)]
    dq_ref, dk_ref, dv_ref, a_ref, x_ref, dm_ref, wq_hbm, wk_hbm, wv_hbm = take(9)
    vec_ref, early_ref = take(2)
    ig_ref, gq_ref, gk_ref, gv_ref, total_ref = take(5)
    wq_ref, wk_ref, wv_ref, away_ref, own_ref, got_ref, back_ref = take(7)
    sums_ref, heard_ref, load_sem, send_sem, recv_sem = take(5)
    place = Place(seq_size)
    links = Links(place, send_sem, recv_sem)
    rows, width = a_ref.shape
    half, split = rows // 2, width // 2
    loads = [
        pltpu.make_async_copy(hbm, ref, load_sem.at[i])
        for i, (hbm, ref) in enumerate(((wq_hbm, wq_ref), (wk_hbm, wk_ref), (wv_hbm, wv_ref)))
    ]
    for load in loads:
        load.start()
    items = {}
    for i, (name, out) in enumerate((("V", gv_ref), ("K", gk_ref), ("Q", gq_ref))):
        first = name == "K"
        writer = column_writer(out, place, 0, split, split)
        items[name] = Item(links, own_ref.at[i], take(6), first, writer)
    shares = [links.copy(away_ref.at[i], got_ref.at[i], "core") for i in range(3)]
    ig_swap = links.copy(back_ref, ig_ref.at[place.chip], "x")
    ways = ("core", "x", 0, 1, 2)
    tells = [links.copy(sums_ref.at[i], heard_ref.at[i], way) for i, way in enumerate(ways)]
    greet(place, ways)
    mine = pl.ds(pl.multiple_of(place.core * split, 128), split)
    away = pl.ds(pl.multiple_of((1 - place.core) * split, 128), split)
    shape = own_ref.shape[1:]

    def grow(i, ref):
        far = dot_tt(a_ref[...], ref[away, :])
        away_ref[i] = far.astype(BF16).reshape(shape)
        own_ref[i] = dot_tt(a_ref[...], ref[mine, :]).astype(BF16).reshape(shape)
        shares[i].start()

    def launch(i, name):
        shares[i].wait_recv()
        add_to(own_ref.at[i], got_ref.at[i])
        items[name].step(0)

    gain = vector(vec_ref, GAIN_1)
    totals = []

    def input_rows(part):
        span = slice(part * half, (part + 1) * half)
        grad = dot_tt(dq_ref[:, span], wq_ref[...])
        grad = grad + dot_tt(dk_ref[:, span], wk_ref[...])
        grad = grad + dot_tt(dv_ref[:, span], wv_ref[...])
        hat, scale = norm_parts(x_ref[span, :].astype(F32))
        totals.append(
            (
                jnp.sum(grad * hat, axis=0, keepdims=True),
                jnp.sum(grad, axis=0, keepdims=True),
            )
        )
        return (dm_ref[span, :] + norm_back(hat, scale, gain, grad)).astype(BF16)

    grow(0, dv_ref)
    grow(1, dk_ref)
    launch(0, "V")
    grow(2, dq_ref)
    launch(1, "K")
    for load in loads:
        load.wait()
    back_ref[...] = input_rows(1)
    launch(2, "Q")
    ig_swap.start()
    ones = jnp.ones((8, rows), BF16)
    sums_ref[0] = early_ref[...]
    sums_ref[0, B_QUERY : B_QUERY + 1, :] = dot_nt(ones, dq_ref[...])[0:1]
    sums_ref[0, B_VALUE : B_VALUE + 1, :] = dot_nt(ones, dv_ref[...])[0:1]
    ig_ref[place.chip] = input_rows(0)
    sums_ref[0, GAIN_1 : GAIN_1 + 1, :] = totals[0][0] + totals[1][0]
    sums_ref[0, BIAS_1 : BIAS_1 + 1, :] = totals[0][1] + totals[1][1]
    for name, step in LATE_PLAN:
        if name != "sum":
            items[name].step(step)
            continue
        if step > 0:
            tells[step - 1].wait_recv()
            both = sums_ref[step - 1] + heard_ref[step - 1]
            if step < len(ways):
                sums_ref[step] = both
            else:
                total_ref[...] = both
        if step < len(ways):
            tells[step].start()
    ig_swap.wait()
    for copy in shares + tells:
        copy.wait_send()
    for name in ("V", "K", "Q"):
        items[name].finish()


def late(seq_size, dq, dk, dv, a, x, dm, wq, wk, wv, vectors, early):
    rows, width = a.shape
    shape = jax.ShapeDtypeStruct
    split, chunk = width // 2, width // GROUPS
    buffers = []
    for first in (False, True, False):
        buffers += item_buffers(chunk, split, first)
    copies = 5 + 6 + 5 + 3 + 1 + 5
    block = (3, 2, 2, 2, chunk, split)
    return pl.pallas_call(
        functools.partial(late_kernel, seq_size),
        out_shape=(
            shape((2, rows // 2, width), BF16),
            shape((chunk, width), F32),
            shape((chunk, width), F32),
            shape((chunk, width), F32),
            shape((VECTORS, width), F32),
        ),
        in_specs=[vmem_spec()] * 6 + [any_spec()] * 3 + [vmem_spec()] * 2,
        out_specs=[vmem_spec()] * 5,
        scratch_shapes=[
            pltpu.VMEM((width, width), BF16),
            pltpu.VMEM((width, width), BF16),
            pltpu.VMEM((width, width), BF16),
            pltpu.VMEM(block, BF16),
            pltpu.VMEM(block, BF16),
            pltpu.VMEM(block, BF16),
            pltpu.VMEM((rows // 2, width), BF16),
            pltpu.VMEM((5, VECTORS, width), F32),
            pltpu.VMEM((5, VECTORS, width), F32),
            pltpu.SemaphoreType.DMA((3,)),
            pltpu.SemaphoreType.DMA((copies,)),
            pltpu.SemaphoreType.DMA((copies,)),
        ]
        + buffers,
        compiler_params=pltpu.CompilerParams(collective_id=3, has_side_effects=True),
        name="late",
    )(dq, dk, dv, a, x, dm, wq, wk, wv, vectors, early)


def layer_norm(inputs, gain_vec, bias_vec):
    centre = jnp.mean(inputs, axis=-1, keepdims=True)
    centred = inputs - centre
    spread = jnp.mean(centred * centred, axis=-1, keepdims=True)
    return centred * lax.rsqrt(spread + EPSILON) * gain_vec + bias_vec


def middle(x, attended, cotangent, wout, wup, wdown, vectors):
    rows, width = x.shape
    vec = vectors.astype(F32)
    stream = x.astype(F32) + dot_tn(attended, wout) + vec[B_OUT]
    normed = layer_norm(stream, vec[GAIN_2], vec[BIAS_2]).astype(BF16)
    pre = dot_nn(normed, wup) + vec[B_UP : B_UP + 4].reshape(-1)
    hidden, pull = jax.vjp(lambda inner: jax.nn.gelu(inner, approximate=False), pre)
    hidden = hidden.astype(BF16)
    result = (stream + dot_nn(hidden, wdown) + vec[B_DOWN]).astype(BF16)
    grad_down = dot_tn(hidden, cotangent).astype(BF16)
    (dpre,) = pull(dot_nt(cotangent, wdown))
    sum_up = jnp.sum(dpre, axis=0)
    dpre = dpre.astype(BF16)
    grad_up = dot_tn(normed, dpre).astype(BF16)
    dnormed = dot_nt(dpre, wup)
    _, pull = jax.vjp(layer_norm, stream, vec[GAIN_2], vec[BIAS_2])
    dstream, sum_gain, sum_bias = pull(dnormed)
    dstream = cotangent.astype(F32) + dstream
    branch = dstream.astype(BF16)
    grad_out = dot_nn(attended, branch).astype(BF16)
    dattended = dot_nt(wout, branch).astype(BF16)
    delta = jnp.sum(
        (dattended.astype(F32) * attended.astype(F32)).reshape(HEADS, HEAD_DIM, rows),
        axis=1,
        keepdims=True,
    )
    zero = jnp.zeros((1, width), F32)
    early = {
        B_OUT: jnp.sum(branch.astype(F32), axis=0)[None],
        GAIN_2: sum_gain[None],
        BIAS_2: sum_bias[None],
        B_DOWN: jnp.sum(cotangent.astype(F32), axis=0)[None],
        B_UP: sum_up.reshape(4, width),
    }
    pieces = [early.get(row, zero) for row in range(B_UP + 1)]
    pieces.append(jnp.zeros((VECTORS - B_UP - 4, width), F32))
    early = jnp.concatenate(pieces, axis=0)

    def cores(grad, count):
        high, wide = grad.shape
        columns = wide // 2 // count
        whole = grad.reshape(GROUPS, high // GROUPS, 2, count, columns)
        whole = whole.transpose(2, 3, 0, 1, 4)
        core = lax.axis_index("band") % 2
        away = lax.dynamic_index_in_dim(whole, 1 - core, 0, keepdims=False)
        mine = lax.dynamic_index_in_dim(whole, core, 0, keepdims=False)
        got = lax.ppermute(away, "band", [(i, i ^ 1) for i in range(4)])
        both = (mine.astype(F32) + got.astype(F32)).astype(BF16)
        return both.reshape(count, 2, 2, 2, high // GROUPS, columns)

    down = cores(grad_down, DOWN_PIECES)
    up = cores(grad_up, UP_PIECES)
    out = cores(grad_out, 1)[0]
    return result, dstream, dattended, delta, early, down, up, out


def body(
    tokens,
    slot_ids,
    cotangent,
    ln1_gain,
    ln1_bias,
    w_query,
    b_query,
    w_key,
    w_value,
    b_value,
    w_out,
    b_out,
    ln2_gain,
    ln2_bias,
    w_up,
    b_up,
    w_down,
    b_down,
):
    seq_size = lax.axis_size("seq")
    shape = tokens.shape
    width = shape[-1]
    flat = (shape[0], -1, width)
    singles = [ln1_gain, ln1_bias, b_query, b_value, b_out, ln2_gain, ln2_bias, b_down, b_up]
    vectors = jnp.concatenate(singles + [jnp.zeros((4 * width,), BF16)]).reshape(VECTORS, width)
    x, g, a, q, k, v, o, lse = front(
        seq_size,
        tokens.reshape(flat),
        cotangent.reshape(flat),
        w_query,
        w_key,
        w_value,
        vectors,
        slot_ids,
    )
    result, dm, do, delta, early, down, up, out = middle(x, o, g, w_out, w_up, w_down, vectors)
    dq, dk, dv, result, g_down, g_up, g_out = back(
        seq_size, slot_ids, q, k, v, do, lse, delta, result, down, up, out
    )
    input_grad, g_query, g_key, g_value, sums = late(
        seq_size, dq, dk, dv, a, x, dm, w_query, w_key, w_value, vectors, early
    )
    extra = seq_size // GROUPS
    grads = [g_query, g_key, g_value, g_out, g_up, g_down]
    if extra > 1:
        groups = [[g * extra + i for i in range(extra)] for g in range(GROUPS)]
        grads = [
            lax.psum_scatter(
                grad, "seq", scatter_dimension=0, axis_index_groups=groups, tiled=True
            )
            for grad in grads
        ]
        sums = lax.psum(sums, "seq", axis_index_groups=groups)
    g_query, g_key, g_value, g_out, g_up, g_down = grads
    place = lax.axis_index("seq")
    share = width // seq_size

    def part(row):
        return lax.dynamic_slice(sums, (row, place * share), (1, share)).reshape(share)

    up_share = b_up.shape[0] // seq_size
    g_b_up = lax.dynamic_slice(
        sums[B_UP : B_UP + 4].reshape(-1), (place * up_share,), (up_share,)
    )
    return (
        result.reshape(shape),
        input_grad.reshape(shape),
        part(GAIN_1),
        part(BIAS_1),
        g_query,
        part(B_QUERY),
        g_key,
        g_value,
        part(B_VALUE),
        g_out,
        part(B_OUT),
        part(GAIN_2),
        part(BIAS_2),
        g_up,
        g_b_up,
        g_down,
        part(B_DOWN),
    )


def solution(mesh):
    row = P("seq", None)
    vec = P("seq")
    whole = P("seq", None, "band", None, None)
    in_specs = (whole, row, whole) + (P(),) * 15
    out_specs = (
        whole,
        whole,
        vec,
        vec,
        row,
        vec,
        row,
        row,
        vec,
        row,
        vec,
        vec,
        vec,
        row,
        vec,
        row,
        vec,
    )
    return jax.shard_map(body, mesh=mesh, in_specs=in_specs, out_specs=out_specs, check_vma=False)
```
